32 devices in a mesh: groups: 2 (over y), blocks: 4 (over z), tiles: 2 (over x), sub: 2 (over core).
Axes of the slice: x: 2, y: 2, z: 4, core: 2. Of those that a mesh axis runs over, the one named last changes fastest.
Arguments:
- seg_feat: bfloat16 [8, 4, 2048, 128], P(('groups', 'tiles', 'sub'), 'blocks'), parts along dimension 0, may hold values from -6 to 6
- seg_block: int32 [8, 4, 2048, 1], P(('groups', 'tiles', 'sub'), 'blocks'), parts along dimension 0, may hold values from 0 to 3; in each aligned block of 2048 rows (0 to 2047, 2048 to 4095, ..., all dimensions but the last counted through in order) at most 1024 rows name the same one
- depth_rank: int32 [8, 4, 8, 256], P(('groups', 'tiles', 'sub'), 'blocks'), parts along dimension 0, may hold values from 0 to 7, as said below
- w_in: bfloat16 [4, 128, 512], P('blocks'), may hold values from -0.5 to 0.5
- w_hidden: bfloat16 [4, 4, 512, 512], P('blocks'), may hold values from -0.25 to 0.25
- w_out: bfloat16 [4, 512, 128], P('blocks'), may hold values from -0.25 to 0.25
- w_dens: bfloat16 [4, 512], P('blocks'), may hold values from -0.25 to 0.25
- conv_w: bfloat16 [3, 3, 3, 128, 128], replicated, may hold values from -0.1875 to 0.1875
Outputs:
- decoded: bfloat16 [128, 64, 128], P(('groups', 'tiles', 'sub'), 'blocks'), parts along dimension 0
The draws below stay inside these ranges and needn't reach their ends.
There are 2 independent parts, one for each index of `groups`. The reference program is written for one: setup_inputs(seed, part) draws one part's arguments, and reference() takes and returns one part's arrays. A program takes and returns all parts, laid end to end along the dimension named above; an argument that names none is the same for every part. Nothing has to cross between parts.
Inputs may be any that keep to these rules, and one draw needn't show every extreme that they name: `seg_block`: among one device's 2048 segments, no block is named more than 1024 times; some device names some block exactly 1024 times. `depth_rank`: for every ray, its 8 segments' ranks are a permutation of 0 .. 7.
All inputs are finite; a program needn't handle non-finite values.
Results may differ from the reference program's by a relative error of at most 0.02.
Values may be sent and summed in bfloat16 or wider, within the bound.
No kernel may reach another device: no remote copies, remote signals or barrier semaphores. Data moves between devices by JAX's collectives and lax.ppermute only.
A program may use at most 64 MiB of HBM per device.

```python
import math
import jax
import jax.numpy as jnp
import numpy as np
from jax import lax

F_IN = 128
HID = 512
FEAT = 128
LAYERS = 4
SEGS_RAY = 8
CONV_LAYERS = 3
TW = 16
TH = 16
RAYS_DEV = 256
SEG_DEV = 2048
CAP = 1024
RT = 4
N_BLOCKS = 4


def draw_depth_rank(key, part):
    scores = jax.random.randint(key, (RT, N_BLOCKS, SEGS_RAY, RAYS_DEV), 0, 1 << 20) * SEGS_RAY
    scores = scores + jnp.arange(SEGS_RAY, dtype=jnp.int32)[:, None]
    ordering = jnp.argsort(scores, axis=2)
    return jnp.argsort(ordering, axis=2).astype(jnp.int32)


def steps_of(rng, shape, split, smallest, largest):
    def one(axis_at, blocks):
        steps = jax.random.uniform(jax.random.fold_in(jax.random.fold_in(rng, 6), axis_at), (blocks,), jnp.float32, smallest / len(split), largest / len(split))
        return jnp.repeat(jnp.exp(steps), shape[axis_at] // blocks).reshape((-1,) + (1,) * (len(shape) - axis_at - 1))

    gain = one(*split[0])
    for cut in split[1:]:
        gain = gain * one(*cut)
    return gain


def deal_out(rng, own, number, rows, amount, top, most, skew):
    ranking = jax.random.permutation(rng, amount)
    crowded, usual = load_shares(amount, rows * top, most, skew, True), load_shares(amount, rows * top, most, skew, False)
    places = jnp.arange(amount)

    def named(lengths, turn):
        used = int((lengths > 0).sum())
        fixed = max(1, used // 4)
        shifted = fixed + (places - fixed + turn * (used - fixed)) % max(1, amount - fixed)
        return jnp.zeros((amount,), jnp.int32).at[ranking[jnp.where(places < fixed, places, shifted)]].set(jnp.asarray(lengths, jnp.int32))

    lengths = jnp.where(number % 4 == 0, named(crowded, number // 4), named(usual, number - number // 4 - 1))
    mixed = jax.random.permutation(jax.random.fold_in(own, 3), amount)
    donor, receiver = mixed[0:amount // 2 * 2:2], mixed[1:amount // 2 * 2:2]
    slack = jnp.minimum(lengths[donor] - 1, most - lengths[receiver]) // 2
    slack = jnp.where((donor == ranking[0]) | (receiver == ranking[0]) | (lengths[receiver] == 0), 0, jnp.maximum(slack, 0))
    shifted = jax.random.randint(jax.random.fold_in(own, 4), (amount // 2,), 0, 1 << 20) % (slack + 1)
    lengths = lengths.at[donor].add(-shifted).at[receiver].add(shifted)
    labels = jnp.searchsorted(jnp.cumsum(lengths), jnp.arange(rows * top), side="right").astype(jnp.int32)
    grid = labels.reshape(top, rows).T
    grid = grid[jax.random.permutation(jax.random.fold_in(own, 1), rows)]
    turn = jax.random.randint(jax.random.fold_in(own, 2), (rows, 1), 0, top)
    return jnp.take_along_axis(grid, (jnp.arange(top)[None, :] + turn) % top, axis=1)


def load_shares(count, total, most, lean, full):
    portions = [(1 << 20) // math.isqrt(grade ** lean) + 1 for grade in range(1, count + 1)]
    largest = most if full else min(most, max(-(-total // count), total * portions[0] // sum(portions)))
    least = 1 if total - largest >= count - 1 else 0
    holding, spare = [largest] + [least] * (count - 1), total - largest - least * (count - 1)
    while spare > 0:
        free = [i for i in range(1, count) if holding[i] < largest] or [i for i in range(1, count) if holding[i] < most]
        mass, remaining = sum([portions[i] for i in free]), spare
        for i in free:
            extra = min(most - holding[i], max(1, remaining * portions[i] // mass), spare)
            holding[i] = holding[i] + extra
            spare = spare - extra
    return np.array(holding)


def noise(stream_key, shape, deviation, most, cuts=(), kind=jnp.bfloat16):
    factor_of = steps_of(stream_key, shape, cuts, -0.22, 0.18) if cuts else 1.0
    entries = jax.random.normal(stream_key, shape, jnp.float32) * deviation * factor_of
    return jnp.minimum(jnp.maximum(entries, -most), most).astype(kind)


def setup_inputs(seed: int = 0, part: int = 0) -> dict:
    key_of = jax.random.split(jax.random.key(seed), 9)
    part_keys = jax.random.split(jax.random.fold_in(key_of[8], part), 9)
    seg_feat = noise(part_keys[0], (RT, N_BLOCKS, SEG_DEV, F_IN), 1.0, 6.0, ((0, 4), (1, 4)))
    seg_block_keys = jax.random.split(jax.random.fold_in(part_keys[1], 1), RT * N_BLOCKS * SEG_DEV // SEG_DEV)
    seg_block_turns = jax.random.permutation(jax.random.fold_in(part_keys[1], 3), RT * N_BLOCKS * SEG_DEV // SEG_DEV)
    seg_block = jax.vmap(lambda own, number: deal_out(jax.random.fold_in(part_keys[1], 2), own, number, SEG_DEV, N_BLOCKS, 1, CAP, 2))(seg_block_keys, seg_block_turns).reshape((RT, N_BLOCKS, SEG_DEV, 1))
    depth_rank = draw_depth_rank(jax.random.fold_in(jax.random.fold_in(key_of[8], part), 71), part)
    w_in = noise(key_of[3], (N_BLOCKS, F_IN, HID), F_IN ** -0.5, 0.5, ((0, 4),))
    w_hidden = noise(key_of[4], (N_BLOCKS, LAYERS, HID, HID), HID ** -0.5, 0.25, ((0, 4),))
    w_out = noise(key_of[5], (N_BLOCKS, HID, FEAT), HID ** -0.5, 0.25, ((0, 4),))
    w_dens = noise(key_of[6], (N_BLOCKS, HID), HID ** -0.5, 0.25, ((0, 4),))
    conv_w = noise(key_of[7], (CONV_LAYERS, 3, 3, FEAT, FEAT), (9 * FEAT) ** -0.5, 0.1875)
    return dict(seg_feat=seg_feat, seg_block=seg_block, depth_rank=depth_rank, w_in=w_in, w_hidden=w_hidden, w_out=w_out, w_dens=w_dens, conv_w=conv_w)


def place_rows(block_ids, capacity, block_count):
    onehot = (block_ids[:, None] == jnp.arange(block_count, dtype=jnp.int32)[None, :]).astype(jnp.int32)
    before = jnp.cumsum(onehot, axis=0) - onehot
    return (block_ids * capacity + jnp.sum(before * onehot, axis=1)).astype(jnp.int32)


def evaluate(row_block, first_weight, hidden, last_weight, density_row):
    hidden_act = jax.nn.silu(jnp.dot(row_block, first_weight, preferred_element_type=jnp.float32)).astype(jnp.bfloat16)
    for layer_index in range(hidden.shape[0]):
        update = jax.nn.silu(jnp.dot(hidden_act, hidden[layer_index], preferred_element_type=jnp.float32))
        hidden_act = (hidden_act.astype(jnp.float32) + update).astype(jnp.bfloat16)
    features = jnp.dot(hidden_act, last_weight, preferred_element_type=jnp.float32).astype(jnp.bfloat16)
    raw_density = jnp.dot(hidden_act, density_row, preferred_element_type=jnp.float32)
    density = (0.25 * jax.nn.softplus(raw_density)).astype(jnp.bfloat16)
    return features, density


def composite(features, density, rank_table):
    density_f32 = density.astype(jnp.float32)
    in_front = (rank_table[:, None, :] < rank_table[None, :, :]).astype(jnp.float32)
    optical = jnp.sum(density_f32[:, None, :] * in_front, axis=0)
    weight = jnp.exp(-optical) * (1.0 - jnp.exp(-density_f32))
    pixel_color = jnp.sum(weight[:, :, None] * features.astype(jnp.float32), axis=0)
    return pixel_color.astype(jnp.bfloat16)


def conv_layer(padded, kernel, out_rows, out_cols):
    pieces = []
    for offset_y in range(3):
        for offset_x in range(3):
            pieces.append(padded[offset_y:offset_y + out_rows, offset_x:offset_x + out_cols])
    patches = jnp.concatenate(pieces, axis=-1)
    channels = kernel.shape[-1]
    result = jnp.dot(patches, kernel.reshape(9 * kernel.shape[2], channels), preferred_element_type=jnp.float32)
    center = padded[1:1 + out_rows, 1:1 + out_cols].astype(jnp.float32)
    return (center + jax.nn.silu(result)).astype(jnp.bfloat16)


def reference(seg_feat, seg_block, depth_rank, w_in, w_hidden, w_out, w_dens, conv_w):
    block_table = seg_block[..., 0]
    slot_index = jax.vmap(jax.vmap(lambda block_ids: place_rows(block_ids, CAP, N_BLOCKS)))(block_table)

    def fill_rows(row_block, positions):
        return jnp.zeros((N_BLOCKS * CAP, F_IN), jnp.bfloat16).at[positions].set(row_block)

    sendbuf = jax.vmap(jax.vmap(fill_rows))(seg_feat, slot_index).reshape(RT, N_BLOCKS, N_BLOCKS, CAP, F_IN)

    def per_block(block_id):
        row_block = sendbuf[:, :, block_id].reshape(RT * N_BLOCKS * CAP, F_IN)
        features, density = evaluate(row_block, w_in[block_id], w_hidden[block_id], w_out[block_id], w_dens[block_id])
        return features.reshape(RT, N_BLOCKS, CAP, FEAT), density.reshape(RT, N_BLOCKS, CAP)

    feat_all, density_all = lax.map(per_block, jnp.arange(N_BLOCKS, dtype=jnp.int32))
    feat_back = feat_all.transpose(1, 2, 0, 3, 4).reshape(RT, N_BLOCKS, N_BLOCKS * CAP, FEAT)
    density_back = density_all.transpose(1, 2, 0, 3).reshape(RT, N_BLOCKS, N_BLOCKS * CAP)

    def finish(feat_rows, density_rows, positions, rank_table):
        feat_seg = feat_rows[positions].reshape(SEGS_RAY, RAYS_DEV, FEAT)
        density_seg = density_rows[positions].reshape(SEGS_RAY, RAYS_DEV)
        return composite(feat_seg, density_seg, rank_table)

    colors = jax.vmap(jax.vmap(finish))(feat_back, density_back, slot_index, depth_rank)
    image_map = colors.reshape(RT, N_BLOCKS, TH, TW, FEAT).transpose(0, 2, 1, 3, 4).reshape(RT * TH, N_BLOCKS * TW, FEAT)
    for layer_index in range(CONV_LAYERS):
        padded = jnp.pad(image_map, ((1, 1), (1, 1), (0, 0)))
        image_map = conv_layer(padded, conv_w[layer_index], RT * TH, N_BLOCKS * TW)
    return image_map
```

```python
import functools

import jax
import jax.numpy as jnp
from jax import lax
from jax.experimental import pallas as pl
from jax.experimental.pallas import tpu as pltpu
from jax.sharding import PartitionSpec as P

SEGS_RAY = 8
CONV_LAYERS = 3
TW = 16
TH = 16
RAYS_DEV = 256
LANES = 128
ALIGN = 16
EDGE = CONV_LAYERS * TH

F32 = jnp.float32
BF16 = jnp.bfloat16
I32 = jnp.int32


def iota(shape, dim):
    return lax.broadcasted_iota(I32, shape, dim)


def dot(a, b):
    return jnp.dot(a, b, preferred_element_type=F32)


def dot_nt(a, b):
    return lax.dot_general(a, b, (((1,), (1,)), ((), ())), preferred_element_type=F32)


def dot_tn(a, b):
    return lax.dot_general(a, b, (((0,), (0,)), ((), ())), preferred_element_type=F32)


def silu(x):
    z = 0.5 * x
    return z + z * jnp.tanh(z)


def meta_rows(capacity):
    return -(-capacity // (8 * LANES)) * 8


def pack_kernel(count, capacity, me_ref, feat_ref, block_ref, rank_ref, *rest):
    outs, packed = rest[:count], rest[count]
    me = me_ref[0]
    segments = feat_ref.shape[0]
    rows = segments // LANES
    tiles = segments // RAYS_DEV
    per_tile = RAYS_DEV // LANES
    window = RAYS_DEV + ALIGN

    target = block_ref[...] ^ me
    onehot = jnp.concatenate([(target == d).astype(F32) for d in range(count)], axis=0)
    onehot_b = onehot.astype(BF16)
    upper = (iota((LANES, LANES), 0) <= iota((LANES, LANES), 1)).astype(F32).astype(BF16)
    within = dot(onehot_b, upper)
    total = dot(onehot_b, jnp.ones((LANES, LANES), BF16))
    size = count * rows
    r_i, c_i = iota((size, size), 0), iota((size, size), 1)
    first = r_i - lax.rem(r_i, rows)
    earlier = ((c_i < r_i) & (c_i >= first)).astype(F32).astype(BF16)
    start = dot(earlier, total.astype(BF16))
    position = within - 1.0 + start
    start_i = start.astype(I32)

    rank_t = jnp.transpose(rank_ref[...].astype(F32))
    ray_col = iota((RAYS_DEV, LANES), 0).astype(F32)
    odd = (iota((RAYS_DEV, LANES), 1) & 1) == 1
    slot_iota = iota((window, RAYS_DEV), 0).astype(F32)
    for d in range(count):
        packed[d, 0:ALIGN, :] = jnp.zeros((ALIGN, 2 * LANES), BF16)
    for j in range(tiles):
        rank_col = jnp.broadcast_to(rank_t[:, j : j + 1] + 1.0, (RAYS_DEV, LANES))
        extra = jnp.where(odd, rank_col, ray_col).astype(BF16)
        source = jnp.concatenate([feat_ref[j * RAYS_DEV : (j + 1) * RAYS_DEV, :], extra], axis=1)
        for d in range(count):
            row = d * rows + j * per_tile
            base_vec = start_i[row : row + 1, :] & (-ALIGN)
            base = pl.multiple_of(jnp.max(base_vec), ALIGN)
            base_f = base_vec.astype(F32)
            pieces = []
            for i in range(per_tile):
                hit = onehot[row + i : row + i + 1, :] > 0.5
                pieces.append(jnp.where(hit, position[row + i : row + i + 1, :] - base_f, -1.0))
            key = jnp.concatenate(pieces, axis=1)
            select = jnp.where(slot_iota == key, 1.0, 0.0).astype(BF16)
            moved = dot(select, source).astype(BF16)
            head = packed[d, pl.ds(base, ALIGN), :] + moved[:ALIGN]
            packed[d, pl.ds(base, ALIGN), :] = head
            packed[d, pl.ds(base + ALIGN, RAYS_DEV), :] = moved[ALIGN:]

    lane_pair = iota((capacity, LANES), 1) >> 1
    info = jnp.zeros((capacity, LANES), F32)
    valid_row = iota((capacity, LANES), 0)
    for d in range(count):
        last = d * rows + rows - 1
        filled = jnp.max((start + total)[last : last + 1, :].astype(I32))
        piece = packed[d, 0:capacity, LANES:].astype(F32)
        keep = (lane_pair == d) & (valid_row < filled)
        info = jnp.where(keep, piece, info)
        outs[d][0:capacity, :] = jnp.where(
            valid_row < filled, packed[d, 0:capacity, :LANES].astype(F32), 0.0
        ).astype(BF16)
    info_t = jnp.transpose(info)
    blocks = capacity // LANES
    mrows = meta_rows(capacity)
    for d in range(count):
        parts = []
        for which in range(2):
            line = info_t[2 * d + which : 2 * d + which + 1, :]
            parts += [line[:, i * LANES : (i + 1) * LANES] for i in range(blocks)]
            if mrows > blocks:
                parts.append(jnp.zeros((mrows - blocks, LANES), F32))
        outs[d][capacity:, :] = jnp.concatenate(parts, axis=0).astype(BF16)


def slot_lines(info, capacity):
    blocks = capacity // LANES
    mrows = meta_rows(capacity)
    ray = jnp.concatenate([info[i : i + 1, :] for i in range(blocks)], axis=1)
    rank = jnp.concatenate([info[mrows + i : mrows + i + 1, :] for i in range(blocks)], axis=1)
    return ray, rank


def mlp_kernel(capacity, tile, prior, *refs):
    message, w_in, w_hidden, w_out, w_dens = refs[:5]
    earlier = refs[5 : 5 + prior]
    feat_out, dens_out = refs[5 + prior : 7 + prior]
    hid = w_in.shape[1]
    layers = w_hidden.shape[0]
    tiles = capacity // tile
    acts = [
        silu(dot(message[i * tile : (i + 1) * tile, :], w_in[...])).astype(BF16)
        for i in range(tiles)
    ]
    for layer in range(layers):
        for i in range(tiles):
            update = silu(dot(acts[i], w_hidden[layer]))
            acts[i] = (acts[i].astype(F32) + update).astype(BF16)
    w_line = jnp.broadcast_to(w_dens[...].astype(F32), (8, hid)).astype(BF16)
    raws = [dot_nt(w_line, acts[i]) for i in range(tiles)]
    raw = jnp.concatenate(raws, axis=1)
    softplus = jnp.maximum(raw, 0.0) + jnp.log1p(jnp.exp(-jnp.abs(raw)))
    density = (0.25 * softplus).astype(BF16).astype(F32)
    ray, rank = slot_lines(message[capacity:, :].astype(F32), capacity)
    rank_hit = (rank - 1.0) == iota((SEGS_RAY, capacity), 0).astype(F32)
    by_rank = jnp.where(rank_hit, density[:SEGS_RAY], 0.0).astype(BF16)
    by_ray = jnp.where(iota((RAYS_DEV, capacity), 0).astype(F32) == ray, 1.0, 0.0).astype(BF16)
    table = dot_nt(by_rank, by_ray)
    parts = [e[...] for e in earlier] + [table]
    dens_out[...] = jnp.concatenate(parts, axis=0).astype(dens_out.dtype)
    for i in range(tiles):
        feat_out[i * tile : (i + 1) * tile, :] = dot(acts[i], w_out[...]).astype(BF16)


def color_kernel(count, capacity, me_ref, *refs):
    tables = refs[:count]
    feats = refs[count : 2 * count]
    infos = refs[2 * count : 3 * count]
    outs = refs[3 * count : 4 * count]
    edges = refs[4 * count]
    me = me_ref[0]
    size = count * SEGS_RAY
    summed = []
    for f in range(count):
        part = None
        for e in range(count):
            d = f ^ e
            rows = tables[e][d * SEGS_RAY : (d + 1) * SEGS_RAY, :].astype(F32)
            part = rows if part is None else part + rows
        summed.append(part)
    density = jnp.concatenate(summed, axis=0)
    r_i, c_i = iota((size, size), 0), iota((size, size), 1)
    first = r_i - lax.rem(r_i, SEGS_RAY)
    nearer = ((c_i < r_i) & (c_i >= first)).astype(F32).astype(BF16)
    optical = dot(nearer, density.astype(BF16))
    weight = jnp.exp(-optical) * (1.0 - jnp.exp(-density))
    high = weight.astype(BF16).astype(F32)
    low = weight - high
    e_r, e_c = iota((2 * EDGE, RAYS_DEV), 0), iota((2 * EDGE, RAYS_DEV), 1)
    second = (e_r >= EDGE).astype(I32)
    e_i = e_r - second * EDGE
    e_y = e_i // CONV_LAYERS
    e_x = lax.rem(e_i, CONV_LAYERS)
    ray_of = e_y * TW + jnp.where(second == 1, e_x, e_x + TW - CONV_LAYERS)
    pick = (ray_of == e_c).astype(F32).astype(BF16)
    zero_edge = jnp.zeros((2 * EDGE, LANES), BF16)
    edges[0] = zero_edge
    edges[count + 1] = zero_edge
    for f in range(count):
        ray, rank = slot_lines(infos[f][capacity:, :].astype(F32), capacity)
        rank_hit = jnp.where(
            (rank - 1.0) == iota((SEGS_RAY, capacity), 0).astype(F32), 1.0, 0.0
        )
        rank_hit = jnp.concatenate([rank_hit, rank_hit], axis=0).astype(BF16)
        rows = slice(f * SEGS_RAY, (f + 1) * SEGS_RAY)
        both = jnp.concatenate([high[rows], low[rows]], axis=0).astype(BF16)
        spread = dot_tn(both, rank_hit)
        ray_hit = iota((RAYS_DEV, capacity), 0).astype(F32) == ray
        mixing = jnp.where(ray_hit, spread, 0.0).astype(BF16)
        color = dot(mixing, feats[f][...]).astype(BF16)
        outs[f][0:RAYS_DEV, :] = color
        edges[(me ^ f) + 1] = dot(pick, color).astype(BF16)
    for f in range(count):
        place = me ^ f
        outs[f][RAYS_DEV : RAYS_DEV + EDGE, :] = edges[place, 0:EDGE, :]
        outs[f][RAYS_DEV + EDGE :, :] = edges[place + 2, EDGE:, :]


def sum_kernel(count, *refs):
    parts = refs[:count]
    tile_out, first_out, last_out = refs[count:]
    total = parts[0][...].astype(F32)
    for e in range(1, count):
        total = total + parts[e][...].astype(F32)
    tile = total.astype(BF16)
    tile_out[...] = tile
    edge = CONV_LAYERS * TW
    left, right = RAYS_DEV, RAYS_DEV + EDGE
    first_out[...] = jnp.concatenate(
        [tile[0:edge], tile[left : left + ALIGN], tile[right : right + ALIGN]], axis=0
    )
    last_out[...] = jnp.concatenate(
        [
            tile[RAYS_DEV - edge : RAYS_DEV],
            tile[left + EDGE - ALIGN : left + EDGE],
            tile[right + EDGE - ALIGN : right + EDGE],
        ],
        axis=0,
    )


PITCH = 2 * TW
TALL = TH + 2 * CONV_LAYERS


def conv_kernel(place_ref, tile_ref, above_ref, below_ref, w_ref, out_ref, image):
    row0, col0, rows_total, cols_total = (place_ref[i] for i in range(4))
    edge = CONV_LAYERS * TW
    left, right = RAYS_DEV, RAYS_DEV + EDGE
    pool = jnp.concatenate(
        [
            tile_ref[left : left + 2 * EDGE, :],
            above_ref[edge:, :],
            below_ref[edge:, :],
        ],
        axis=0,
    )
    strips = TALL + 1
    s_r, s_c = iota((strips * TW, pool.shape[0]), 0), iota((strips * TW, pool.shape[0]), 1)
    strip = s_r // TW
    sub = lax.rem(s_r, TW)
    is_right = sub < CONV_LAYERS
    is_left = sub >= TW - CONV_LAYERS
    y = jnp.where(is_left, strip - CONV_LAYERS, strip - 1 - CONV_LAYERS)
    i = jnp.where(is_left, sub - (TW - CONV_LAYERS), sub)
    side = jnp.where(is_left, 0, 1)
    inner = side * EDGE + y * CONV_LAYERS + i
    skip = ALIGN - CONV_LAYERS * CONV_LAYERS
    over = 2 * EDGE + side * ALIGN + skip + (y + CONV_LAYERS) * CONV_LAYERS + i
    under = 2 * EDGE + 2 * ALIGN + side * ALIGN + (y - TH) * CONV_LAYERS + i
    want = jnp.where(y < 0, over, jnp.where(y >= TH, under, inner))
    usable = (is_left | is_right) & (y >= -CONV_LAYERS) & (y < TH + CONV_LAYERS)
    want = jnp.where(usable, want, -1)
    place = (want == s_c).astype(F32).astype(BF16)
    borders = dot(place, pool).astype(BF16)
    zeros = jnp.zeros((TW, LANES), BF16)
    image[0:TW, :] = zeros
    for k in range(strips):
        at = k * PITCH + TW
        image[at : at + TW, :] = borders[k * TW : (k + 1) * TW]
        if k < TALL:
            y_k = k - CONV_LAYERS
            if y_k < 0:
                piece = above_ref[k * TW : (k + 1) * TW, :]
            elif y_k >= TH:
                piece = below_ref[(y_k - TH) * TW : (y_k - TH + 1) * TW, :]
            else:
                piece = tile_ref[y_k * TW : (y_k + 1) * TW, :]
            image[(k + 1) * PITCH : (k + 1) * PITCH + TW, :] = piece
    current = image[PITCH : PITCH + TALL * PITCH, :]
    head = image[PITCH - ALIGN : PITCH, :]
    current = jnp.concatenate([head, current], axis=0)
    height = TALL
    for layer in range(CONV_LAYERS):
        height = height - 2
        span = height * PITCH + ALIGN
        stacked = jnp.concatenate(
            [current[dy * PITCH : dy * PITCH + span] for dy in range(3)], axis=1
        )
        kernel = jnp.concatenate(
            [
                jnp.concatenate([w_ref[layer, dy, dx] for dx in range(3)], axis=1)
                for dy in range(3)
            ],
            axis=0,
        )
        full = dot(stacked, kernel)
        total = (
            pltpu.roll(full[:, :LANES], 1, 0)
            + full[:, LANES : 2 * LANES]
            + pltpu.roll(full[:, 2 * LANES :], span - 1, 0)
        )
        center = current[PITCH : PITCH + span].astype(F32)
        value = center + silu(total)
        at = iota((span, LANES), 0)
        y_at = at // PITCH
        x_at = lax.rem(at, PITCH) - TW
        upper = x_at < -(TW // 2)
        y_at = jnp.where(upper, y_at - 1, y_at)
        x_at = jnp.where(upper, x_at + PITCH, x_at)
        margin = CONV_LAYERS - 1 - layer
        y_img = row0 + y_at - margin
        x_img = col0 + x_at
        keep = (y_img >= 0) & (y_img < rows_total) & (x_img >= 0) & (x_img < cols_total)
        current = jnp.where(keep, value, 0.0).astype(BF16)
    for y_k in range(TH):
        at = ALIGN + y_k * PITCH
        out_ref[y_k * TW : (y_k + 1) * TW, :] = current[at : at + TW]


def shards(seg_feat, seg_block, depth_rank, w_in, w_hidden, w_out, w_dens, conv_w):
    count = lax.axis_size("blocks")
    segments, width = seg_feat.shape[2:]
    hid = w_in.shape[2]
    feat = w_out.shape[2]
    layers = w_hidden.shape[1]
    capacity = 2 * segments // count
    length = capacity + 2 * meta_rows(capacity)
    column = lax.axis_index("blocks").astype(I32)
    tile_row = lax.axis_index(("tiles", "sub")).astype(I32)
    me = column.reshape(1)
    smem = pl.BlockSpec(memory_space=pltpu.SMEM)
    vmem = pl.BlockSpec(memory_space=pltpu.VMEM)

    messages = pl.pallas_call(
        functools.partial(pack_kernel, count, capacity),
        out_shape=[jax.ShapeDtypeStruct((length, width), BF16)] * count,
        in_specs=[smem, vmem, vmem, vmem],
        out_specs=[vmem] * count,
        scratch_shapes=[
            pltpu.VMEM((count, capacity + RAYS_DEV + ALIGN, 2 * LANES), BF16)
        ],
        name="pack",
    )(me, seg_feat[0, 0], seg_block.reshape(segments // LANES, LANES), depth_rank[0, 0])

    def swap(value, d):
        return lax.ppermute(value, "blocks", [(i, i ^ d) for i in range(count)])

    received = {0: messages[0]}
    lag = 2
    order = [2, 1, 3] if count == 4 else list(range(1, count))
    for at, d in enumerate(order):
        value = messages[d]
        if at >= lag:
            ahead = order[at - lag]
            value, received[ahead] = lax.optimization_barrier((value, received[ahead]))
        received[d] = swap(value, d)

    sequence = [0, 1, 2, 3] if count == 4 else list(range(count))
    feats, tables = [], []
    flops = 2 * capacity * (width * hid + layers * hid * hid + hid * feat)
    for d in sequence:
        final = d == count - 1
        prior = count - 1 if final else 0
        height = count * SEGS_RAY if final else SEGS_RAY
        features, table = pl.pallas_call(
            functools.partial(mlp_kernel, capacity, min(capacity, 256), prior),
            out_shape=[
                jax.ShapeDtypeStruct((capacity, feat), BF16),
                jax.ShapeDtypeStruct((height, RAYS_DEV), BF16 if final else F32),
            ],
            in_specs=[vmem] * (5 + prior),
            out_specs=[vmem] * 2,
            cost_estimate=pl.CostEstimate(
                flops=flops, bytes_accessed=0, transcendentals=capacity * hid * (layers + 1)
            ),
            name="mlp",
        )(received[d], w_in[0], w_hidden[0], w_out[0], w_dens, *(tables if final else ()))
        feats.append(features)
        tables.append(table)
    local = tables[-1]
    others = [local] + [swap(local, d) for d in range(1, count)]

    height = RAYS_DEV + 2 * EDGE
    partial = pl.pallas_call(
        functools.partial(color_kernel, count, capacity),
        out_shape=[jax.ShapeDtypeStruct((height, feat), BF16)] * count,
        in_specs=[smem] + [vmem] * (3 * count),
        out_specs=[vmem] * count,
        scratch_shapes=[pltpu.VMEM((count + 2, 2 * EDGE, feat), BF16)],
        name="color",
    )(me, *others, *feats, *[received[d] for d in range(count)])
    pieces = [partial[0]] + [swap(partial[d], d) for d in range(1, count)]

    strip = CONV_LAYERS * TW + 2 * ALIGN
    tile, first, last = pl.pallas_call(
        functools.partial(sum_kernel, count),
        out_shape=[
            jax.ShapeDtypeStruct((height, feat), BF16),
            jax.ShapeDtypeStruct((strip, feat), BF16),
            jax.ShapeDtypeStruct((strip, feat), BF16),
        ],
        in_specs=[vmem] * count,
        out_specs=[vmem] * 3,
        name="total",
    )(*pieces)
    vertical = ("tiles", "sub")
    peers = lax.axis_size(vertical)
    above = lax.ppermute(last, vertical, [(i, i + 1) for i in range(peers - 1)])
    below = lax.ppermute(first, vertical, [(i + 1, i) for i in range(peers - 1)])

    where = jnp.stack(
        [tile_row * TH, column * TW, jnp.int32(TH * peers), jnp.int32(TW * count)]
    )
    decoded = pl.pallas_call(
        conv_kernel,
        out_shape=jax.ShapeDtypeStruct((RAYS_DEV, feat), BF16),
        in_specs=[smem] + [vmem] * 4,
        out_specs=vmem,
        scratch_shapes=[pltpu.VMEM(((TALL + 1) * PITCH + PITCH, feat), BF16)],
        name="decode",
    )(where, tile, above, below, conv_w)
    return decoded.reshape(TH, TW, feat)


def solution(mesh):
    in_specs = (
        P(("groups", "tiles", "sub"), "blocks", None, None),
        P(("groups", "tiles", "sub"), "blocks", None, None),
        P(("groups", "tiles", "sub"), "blocks", None, None),
        P("blocks", None, None),
        P("blocks", None, None, None),
        P("blocks", None, None),
        P("blocks", None),
        P(),
    )
    out_specs = P(("groups", "tiles", "sub"), "blocks", None)
    return jax.shard_map(shards, mesh=mesh, in_specs=in_specs, out_specs=out_specs, check_vma=False)
```

```python
import functools

import jax
import jax.numpy as jnp
from jax import lax
from jax.experimental import pallas as pl
from jax.experimental.pallas import tpu as pltpu
from jax.sharding import PartitionSpec as P

SEGS_RAY = 8
CONV_LAYERS = 3
TW = 16
TH = 16
RAYS_DEV = 256
LANES = 128
ALIGN = 16
EDGE = CONV_LAYERS * TH

F32 = jnp.float32
BF16 = jnp.bfloat16
I32 = jnp.int32


def iota(shape, dim):
    return lax.broadcasted_iota(I32, shape, dim)


def dot(a, b):
    return jnp.dot(a, b, preferred_element_type=F32)


def dot_nt(a, b):
    return lax.dot_general(a, b, (((1,), (1,)), ((), ())), preferred_element_type=F32)


def dot_tn(a, b):
    return lax.dot_general(a, b, (((0,), (0,)), ((), ())), preferred_element_type=F32)


def silu(x):
    z = 0.5 * x
    return z + z * jnp.tanh(z)


def grant(mib):
    return pltpu.CompilerParams(vmem_limit_bytes=mib << 20)


def meta_rows(capacity):
    return -(-capacity // (8 * LANES)) * 8


def pack_kernel(count, capacity, me_ref, feat_ref, block_ref, rank_ref, *rest):
    outs, packed = rest[:count], rest[count]
    me = me_ref[0]
    segments = feat_ref.shape[0]
    rows = segments // LANES
    tiles = segments // RAYS_DEV
    per_tile = RAYS_DEV // LANES
    window = RAYS_DEV + ALIGN

    target = block_ref[...] ^ me
    onehot = jnp.concatenate([(target == d).astype(F32) for d in range(count)], axis=0)
    onehot_b = onehot.astype(BF16)
    upper = (iota((LANES, LANES), 0) <= iota((LANES, LANES), 1)).astype(F32).astype(BF16)
    within = dot(onehot_b, upper)
    total = dot(onehot_b, jnp.ones((LANES, LANES), BF16))
    size = count * rows
    r_i, c_i = iota((size, size), 0), iota((size, size), 1)
    first = r_i - lax.rem(r_i, rows)
    earlier = ((c_i < r_i) & (c_i >= first)).astype(F32).astype(BF16)
    start = dot(earlier, total.astype(BF16))
    position = within - 1.0 + start
    start_i = start.astype(I32)

    rank_t = jnp.transpose(rank_ref[...].astype(F32))
    ray_col = iota((RAYS_DEV, LANES), 0).astype(F32)
    odd = (iota((RAYS_DEV, LANES), 1) & 1) == 1
    slot_iota = iota((window, RAYS_DEV), 0).astype(F32)
    for d in range(count):
        packed[d, 0:ALIGN, :] = jnp.zeros((ALIGN, 2 * LANES), BF16)
    for j in range(tiles):
        rank_col = jnp.broadcast_to(rank_t[:, j : j + 1] + 1.0, (RAYS_DEV, LANES))
        extra = jnp.where(odd, rank_col, ray_col).astype(BF16)
        source = jnp.concatenate([feat_ref[j * RAYS_DEV : (j + 1) * RAYS_DEV, :], extra], axis=1)
        for d in range(count):
            row = d * rows + j * per_tile
            base_vec = start_i[row : row + 1, :] & (-ALIGN)
            base = pl.multiple_of(jnp.max(base_vec), ALIGN)
            base_f = base_vec.astype(F32)
            pieces = []
            for i in range(per_tile):
                hit = onehot[row + i : row + i + 1, :] > 0.5
                pieces.append(jnp.where(hit, position[row + i : row + i + 1, :] - base_f, -1.0))
            key = jnp.concatenate(pieces, axis=1)
            select = jnp.where(slot_iota == key, 1.0, 0.0).astype(BF16)
            moved = dot(select, source).astype(BF16)
            head = packed[d, pl.ds(base, ALIGN), :] + moved[:ALIGN]
            packed[d, pl.ds(base, ALIGN), :] = head
            packed[d, pl.ds(base + ALIGN, RAYS_DEV), :] = moved[ALIGN:]

    lane_pair = iota((capacity, LANES), 1) >> 1
    info = jnp.zeros((capacity, LANES), F32)
    valid_row = iota((capacity, LANES), 0)
    for d in range(count):
        last = d * rows + rows - 1
        filled = jnp.max((start + total)[last : last + 1, :].astype(I32))
        piece = packed[d, 0:capacity, LANES:].astype(F32)
        keep = (lane_pair == d) & (valid_row < filled)
        info = jnp.where(keep, piece, info)
        outs[d][0:capacity, :] = jnp.where(
            valid_row < filled, packed[d, 0:capacity, :LANES].astype(F32), 0.0
        ).astype(BF16)
    info_t = jnp.transpose(info)
    blocks = capacity // LANES
    mrows = meta_rows(capacity)
    for d in range(count):
        parts = []
        for which in range(2):
            line = info_t[2 * d + which : 2 * d + which + 1, :]
            parts += [line[:, i * LANES : (i + 1) * LANES] for i in range(blocks)]
            if mrows > blocks:
                parts.append(jnp.zeros((mrows - blocks, LANES), F32))
        outs[d][capacity:, :] = jnp.concatenate(parts, axis=0).astype(BF16)


def slot_lines(info, capacity):
    blocks = capacity // LANES
    mrows = meta_rows(capacity)
    ray = jnp.concatenate([info[i : i + 1, :] for i in range(blocks)], axis=1)
    rank = jnp.concatenate([info[mrows + i : mrows + i + 1, :] for i in range(blocks)], axis=1)
    return ray, rank


def mlp_kernel(capacity, tile, prior, *refs):
    message, w_in, w_hidden, w_out, w_dens = refs[:5]
    earlier = refs[5 : 5 + prior]
    feat_out, dens_out = refs[5 + prior : 7 + prior]
    hid = w_in.shape[1]
    layers = w_hidden.shape[0]
    tiles = capacity // tile
    acts = [
        silu(dot(message[i * tile : (i + 1) * tile, :], w_in[...])).astype(BF16)
        for i in range(tiles)
    ]
    for layer in range(layers):
        for i in range(tiles):
            update = silu(dot(acts[i], w_hidden[layer]))
            acts[i] = (acts[i].astype(F32) + update).astype(BF16)
    w_line = jnp.broadcast_to(w_dens[...].astype(F32), (8, hid)).astype(BF16)
    raws = [dot_nt(w_line, acts[i]) for i in range(tiles)]
    raw = jnp.concatenate(raws, axis=1)
    softplus = jnp.maximum(raw, 0.0) + jnp.log1p(jnp.exp(-jnp.abs(raw)))
    density = (0.25 * softplus).astype(BF16).astype(F32)
    ray, rank = slot_lines(message[capacity:, :].astype(F32), capacity)
    rank_hit = (rank - 1.0) == iota((SEGS_RAY, capacity), 0).astype(F32)
    by_rank = jnp.where(rank_hit, density[:SEGS_RAY], 0.0).astype(BF16)
    by_ray = jnp.where(iota((RAYS_DEV, capacity), 0).astype(F32) == ray, 1.0, 0.0).astype(BF16)
    table = dot_nt(by_rank, by_ray)
    parts = [e[...] for e in earlier] + [table]
    dens_out[...] = jnp.concatenate(parts, axis=0).astype(dens_out.dtype)
    for i in range(tiles):
        feat_out[i * tile : (i + 1) * tile, :] = dot(acts[i], w_out[...]).astype(BF16)


def color_kernel(count, capacity, me_ref, *refs):
    tables = refs[:count]
    feats = refs[count : 2 * count]
    infos = refs[2 * count : 3 * count]
    outs = refs[3 * count : 4 * count]
    edges = refs[4 * count]
    me = me_ref[0]
    size = count * SEGS_RAY
    summed = []
    for f in range(count):
        part = None
        for e in range(count):
            d = f ^ e
            rows = tables[e][d * SEGS_RAY : (d + 1) * SEGS_RAY, :].astype(F32)
            part = rows if part is None else part + rows
        summed.append(part)
    density = jnp.concatenate(summed, axis=0)
    r_i, c_i = iota((size, size), 0), iota((size, size), 1)
    first = r_i - lax.rem(r_i, SEGS_RAY)
    nearer = ((c_i < r_i) & (c_i >= first)).astype(F32).astype(BF16)
    optical = dot(nearer, density.astype(BF16))
    weight = jnp.exp(-optical) * (1.0 - jnp.exp(-density))
    high = weight.astype(BF16).astype(F32)
    low = weight - high
    e_r, e_c = iota((2 * EDGE, RAYS_DEV), 0), iota((2 * EDGE, RAYS_DEV), 1)
    second = (e_r >= EDGE).astype(I32)
    e_i = e_r - second * EDGE
    e_y = e_i // CONV_LAYERS
    e_x = lax.rem(e_i, CONV_LAYERS)
    ray_of = e_y * TW + jnp.where(second == 1, e_x, e_x + TW - CONV_LAYERS)
    pick = (ray_of == e_c).astype(F32).astype(BF16)
    zero_edge = jnp.zeros((2 * EDGE, LANES), BF16)
    edges[0] = zero_edge
    edges[count + 1] = zero_edge
    for f in range(count):
        ray, rank = slot_lines(infos[f][capacity:, :].astype(F32), capacity)
        rank_hit = jnp.where(
            (rank - 1.0) == iota((SEGS_RAY, capacity), 0).astype(F32), 1.0, 0.0
        )
        rank_hit = jnp.concatenate([rank_hit, rank_hit], axis=0).astype(BF16)
        rows = slice(f * SEGS_RAY, (f + 1) * SEGS_RAY)
        both = jnp.concatenate([high[rows], low[rows]], axis=0).astype(BF16)
        spread = dot_tn(both, rank_hit)
        ray_hit = iota((RAYS_DEV, capacity), 0).astype(F32) == ray
        mixing = jnp.where(ray_hit, spread, 0.0).astype(BF16)
        color = dot(mixing, feats[f][...]).astype(BF16)
        outs[f][0:RAYS_DEV, :] = color
        edges[(me ^ f) + 1] = dot(pick, color).astype(BF16)
    for f in range(count):
        place = me ^ f
        outs[f][RAYS_DEV : RAYS_DEV + EDGE, :] = edges[place, 0:EDGE, :]
        outs[f][RAYS_DEV + EDGE :, :] = edges[place + 2, EDGE:, :]


def sum_kernel(count, *refs):
    parts = refs[:count]
    tile_out, first_out, last_out = refs[count:]
    total = parts[0][...].astype(F32)
    for e in range(1, count):
        total = total + parts[e][...].astype(F32)
    tile = total.astype(BF16)
    tile_out[...] = tile
    edge = CONV_LAYERS * TW
    left, right = RAYS_DEV, RAYS_DEV + EDGE
    first_out[...] = jnp.concatenate(
        [tile[0:edge], tile[left : left + ALIGN], tile[right : right + ALIGN]], axis=0
    )
    last_out[...] = jnp.concatenate(
        [
            tile[RAYS_DEV - edge : RAYS_DEV],
            tile[left + EDGE - ALIGN : left + EDGE],
            tile[right + EDGE - ALIGN : right + EDGE],
        ],
        axis=0,
    )


PITCH = 2 * TW
TALL = TH + 2 * CONV_LAYERS


def conv_kernel(place_ref, tile_ref, above_ref, below_ref, w_ref, out_ref, image):
    row0, col0, rows_total, cols_total = (place_ref[i] for i in range(4))
    edge = CONV_LAYERS * TW
    left, right = RAYS_DEV, RAYS_DEV + EDGE
    pool = jnp.concatenate(
        [
            tile_ref[left : left + 2 * EDGE, :],
            above_ref[edge:, :],
            below_ref[edge:, :],
        ],
        axis=0,
    )
    strips = TALL + 1
    s_r, s_c = iota((strips * TW, pool.shape[0]), 0), iota((strips * TW, pool.shape[0]), 1)
    strip = s_r // TW
    sub = lax.rem(s_r, TW)
    is_right = sub < CONV_LAYERS
    is_left = sub >= TW - CONV_LAYERS
    y = jnp.where(is_left, strip - CONV_LAYERS, strip - 1 - CONV_LAYERS)
    i = jnp.where(is_left, sub - (TW - CONV_LAYERS), sub)
    side = jnp.where(is_left, 0, 1)
    inner = side * EDGE + y * CONV_LAYERS + i
    skip = ALIGN - CONV_LAYERS * CONV_LAYERS
    over = 2 * EDGE + side * ALIGN + skip + (y + CONV_LAYERS) * CONV_LAYERS + i
    under = 2 * EDGE + 2 * ALIGN + side * ALIGN + (y - TH) * CONV_LAYERS + i
    want = jnp.where(y < 0, over, jnp.where(y >= TH, under, inner))
    usable = (is_left | is_right) & (y >= -CONV_LAYERS) & (y < TH + CONV_LAYERS)
    want = jnp.where(usable, want, -1)
    place = (want == s_c).astype(F32).astype(BF16)
    borders = dot(place, pool).astype(BF16)
    zeros = jnp.zeros((TW, LANES), BF16)
    image[0:TW, :] = zeros
    for k in range(strips):
        at = k * PITCH + TW
        image[at : at + TW, :] = borders[k * TW : (k + 1) * TW]
        if k < TALL:
            y_k = k - CONV_LAYERS
            if y_k < 0:
                piece = above_ref[k * TW : (k + 1) * TW, :]
            elif y_k >= TH:
                piece = below_ref[(y_k - TH) * TW : (y_k - TH + 1) * TW, :]
            else:
                piece = tile_ref[y_k * TW : (y_k + 1) * TW, :]
            image[(k + 1) * PITCH : (k + 1) * PITCH + TW, :] = piece
    current = image[PITCH : PITCH + TALL * PITCH, :]
    head = image[PITCH - ALIGN : PITCH, :]
    current = jnp.concatenate([head, current], axis=0)
    height = TALL
    for layer in range(CONV_LAYERS):
        height = height - 2
        span = height * PITCH + ALIGN
        stacked = jnp.concatenate(
            [current[dy * PITCH : dy * PITCH + span] for dy in range(3)], axis=1
        )
        kernel = jnp.concatenate(
            [
                jnp.concatenate([w_ref[layer, dy, dx] for dx in range(3)], axis=1)
                for dy in range(3)
            ],
            axis=0,
        )
        full = dot(stacked, kernel)
        total = (
            pltpu.roll(full[:, :LANES], 1, 0)
            + full[:, LANES : 2 * LANES]
            + pltpu.roll(full[:, 2 * LANES :], span - 1, 0)
        )
        center = current[PITCH : PITCH + span].astype(F32)
        value = center + silu(total)
        at = iota((span, LANES), 0)
        y_at = at // PITCH
        x_at = lax.rem(at, PITCH) - TW
        upper = x_at < -(TW // 2)
        y_at = jnp.where(upper, y_at - 1, y_at)
        x_at = jnp.where(upper, x_at + PITCH, x_at)
        margin = CONV_LAYERS - 1 - layer
        y_img = row0 + y_at - margin
        x_img = col0 + x_at
        keep = (y_img >= 0) & (y_img < rows_total) & (x_img >= 0) & (x_img < cols_total)
        current = jnp.where(keep, value, 0.0).astype(BF16)
    for y_k in range(TH):
        at = ALIGN + y_k * PITCH
        out_ref[y_k * TW : (y_k + 1) * TW, :] = current[at : at + TW]


def shards(seg_feat, seg_block, depth_rank, w_in, w_hidden, w_out, w_dens, conv_w):
    count = lax.axis_size("blocks")
    segments, width = seg_feat.shape[2:]
    hid = w_in.shape[2]
    feat = w_out.shape[2]
    layers = w_hidden.shape[1]
    capacity = 2 * segments // count
    length = capacity + 2 * meta_rows(capacity)
    column = lax.axis_index("blocks").astype(I32)
    tile_row = lax.axis_index(("tiles", "sub")).astype(I32)
    me = column.reshape(1)
    smem = pl.BlockSpec(memory_space=pltpu.SMEM)
    vmem = pl.BlockSpec(memory_space=pltpu.VMEM)

    messages = pl.pallas_call(
        functools.partial(pack_kernel, count, capacity),
        out_shape=[jax.ShapeDtypeStruct((length, width), BF16)] * count,
        in_specs=[smem, vmem, vmem, vmem],
        out_specs=[vmem] * count,
        scratch_shapes=[
            pltpu.VMEM((count, capacity + RAYS_DEV + ALIGN, 2 * LANES), BF16)
        ],
        compiler_params=grant(10),
        name="pack",
    )(me, seg_feat[0, 0], seg_block.reshape(segments // LANES, LANES), depth_rank[0, 0])

    def swap(value, d):
        return lax.ppermute(value, "blocks", [(i, i ^ d) for i in range(count)])

    received = {0: messages[0]}
    lag = 2
    order = [2, 1, 3] if count == 4 else list(range(1, count))
    for at, d in enumerate(order):
        value = messages[d]
        if at >= lag:
            ahead = order[at - lag]
            value, received[ahead] = lax.optimization_barrier((value, received[ahead]))
        received[d] = swap(value, d)

    sequence = [0, 1, 2, 3] if count == 4 else list(range(count))
    feats, tables = [], []
    flops = 2 * capacity * (width * hid + layers * hid * hid + hid * feat)
    for d in sequence:
        final = d == count - 1
        prior = count - 1 if final else 0
        height = count * SEGS_RAY if final else SEGS_RAY
        features, table = pl.pallas_call(
            functools.partial(mlp_kernel, capacity, min(capacity, 256), prior),
            out_shape=[
                jax.ShapeDtypeStruct((capacity, feat), BF16),
                jax.ShapeDtypeStruct((height, RAYS_DEV), BF16 if final else F32),
            ],
            in_specs=[vmem] * (5 + prior),
            out_specs=[vmem] * 2,
            cost_estimate=pl.CostEstimate(
                flops=flops, bytes_accessed=0, transcendentals=capacity * hid * (layers + 1)
            ),
            compiler_params=grant(14),
        name="mlp",
        )(received[d], w_in[0], w_hidden[0], w_out[0], w_dens, *(tables if final else ()))
        feats.append(features)
        tables.append(table)
    local = tables[-1]
    others = [local] + [swap(local, d) for d in range(1, count)]

    height = RAYS_DEV + 2 * EDGE
    partial = pl.pallas_call(
        functools.partial(color_kernel, count, capacity),
        out_shape=[jax.ShapeDtypeStruct((height, feat), BF16)] * count,
        in_specs=[smem] + [vmem] * (3 * count),
        out_specs=[vmem] * count,
        scratch_shapes=[pltpu.VMEM((count + 2, 2 * EDGE, feat), BF16)],
        compiler_params=grant(12),
        name="color",
    )(me, *others, *feats, *[received[d] for d in range(count)])
    pieces = [partial[0]] + [swap(partial[d], d) for d in range(1, count)]

    strip = CONV_LAYERS * TW + 2 * ALIGN
    tile, first, last = pl.pallas_call(
        functools.partial(sum_kernel, count),
        out_shape=[
            jax.ShapeDtypeStruct((height, feat), BF16),
            jax.ShapeDtypeStruct((strip, feat), BF16),
            jax.ShapeDtypeStruct((strip, feat), BF16),
        ],
        in_specs=[vmem] * count,
        out_specs=[vmem] * 3,
        compiler_params=grant(4),
        name="total",
    )(*pieces)
    vertical = ("tiles", "sub")
    peers = lax.axis_size(vertical)
    above = lax.ppermute(last, vertical, [(i, i + 1) for i in range(peers - 1)])
    below = lax.ppermute(first, vertical, [(i + 1, i) for i in range(peers - 1)])

    where = jnp.stack(
        [tile_row * TH, column * TW, jnp.int32(TH * peers), jnp.int32(TW * count)]
    )
    decoded = pl.pallas_call(
        conv_kernel,
        out_shape=jax.ShapeDtypeStruct((RAYS_DEV, feat), BF16),
        in_specs=[smem] + [vmem] * 4,
        out_specs=vmem,
        scratch_shapes=[pltpu.VMEM(((TALL + 1) * PITCH + PITCH, feat), BF16)],
        compiler_params=grant(8),
        name="decode",
    )(where, tile, above, below, conv_w)
    return decoded.reshape(TH, TW, feat)


def solution(mesh):
    in_specs = (
        P(("groups", "tiles", "sub"), "blocks", None, None),
        P(("groups", "tiles", "sub"), "blocks", None, None),
        P(("groups", "tiles", "sub"), "blocks", None, None),
        P("blocks", None, None),
        P("blocks", None, None, None),
        P("blocks", None, None),
        P("blocks", None),
        P(),
    )
    out_specs = P(("groups", "tiles", "sub"), "blocks", None)
    return jax.shard_map(shards, mesh=mesh, in_specs=in_specs, out_specs=out_specs, check_vma=False)
```
